512 devices in a mesh: cuts: 8 (over x, core), tile: 64 (over y, z).
Axes of the slice: x: 4, y: 8, z: 8, core: 2. Of those that a mesh axis runs over, the one named last changes fastest.
Arguments:
- trans_real: float32 [8, 16384, 256], P('cuts', 'tile'), may hold values from 0.6 to 1.4
- trans_imag: float32 [8, 16384, 256], P('cuts', 'tile'), may hold values from -1.5 to 1.5
- probe_real: bfloat16 [128, 128], replicated, may hold values from -6 to 6
- probe_imag: bfloat16 [128, 128], replicated, may hold values from -6 to 6
- offsets: int32 [2, 2048], P(None, 'tile'), may hold values from 0 to 128
- pattern_index: int32 [2048], P('tile'), may hold values from 0 to 2047, as said below
- measured: bfloat16 [2048, 128, 128], P('tile'), may hold values from 0.19921875 to 3
Outputs:
- object_grad: float32 [2, 8, 16384, 256], P(None, 'cuts', 'tile')
The draws below stay inside these ranges and needn't reach their ends.
Inputs may be any that keep to these rules, and one draw needn't show every extreme that they name: `pattern_index`: each row of measured is named by exactly one position; row r is stored with tile r // 32. Of the positions of one tile at most 1 have patterns stored with any one tile, and every tile has exactly 1 with some tile.
All inputs are finite; a program needn't handle non-finite values.
Results may differ from the reference program's by a relative error of at most 0.015.
The reference program's roundings to bfloat16 on the way count: a program that leaves them out, or rounds other values in their place, can miss the bound.
Values may be sent and summed in bfloat16 or wider, within the bound.
No kernel may reach another device: no remote copies, remote signals or barrier semaphores. Data moves between devices by JAX's collectives and lax.ppermute only.
A program may use at most 64 MiB of HBM per device.

```python
import math
import jax
import jax.numpy as jnp
from jax import lax

WIN = 128
PATCH = 256
POS_TILE = 32
SLICES = 8
POSITIONS = 2048
N_TILE = 64


def draw_pattern_index(key, part):
    tile_count = N_TILE
    per_tile = POS_TILE
    unit_size = (per_tile + tile_count - 1) // tile_count
    groups = per_tile // unit_size
    key_shift = jax.random.fold_in(key, 23)
    key_order = jax.random.fold_in(key, 37)
    candidates = jnp.arange(tile_count, dtype=jnp.int32)
    ranking = jax.random.permutation(key_shift, tile_count).astype(jnp.int32)
    forced = (candidates == tile_count // 2) | (candidates == 1 % tile_count) | (candidates == tile_count - 1)
    priority = ranking - 3 * tile_count * forced.astype(jnp.int32)
    shifts = jnp.argsort(priority, stable=True)[:groups].astype(jnp.int32)
    ordinal = jnp.arange(per_tile, dtype=jnp.int32)
    member = ordinal // unit_size
    shift_of = jnp.take(shifts, member)
    devices = jnp.arange(tile_count, dtype=jnp.int32)
    owners = (devices[:, None] + shift_of[None, :]) % tile_count
    rows_index = owners * per_tile + ordinal[None, :]
    scores = jax.random.randint(key_order, (tile_count, per_tile), 0, 1 << 20) * per_tile + ordinal[None, :]
    order_rows = jnp.argsort(scores, axis=1, stable=True)
    shuffled = jnp.take_along_axis(rows_index, order_rows, axis=1)
    return shuffled.reshape(-1).astype(jnp.int32)


def set_ends(drawn, own_key, low, high):
    shape = drawn.shape
    place = [jax.random.randint(jax.random.fold_in(own_key, axis), (), 0, shape[axis]) for axis in range(len(shape))]
    drawn = drawn.at[tuple(place)].set(low)
    longest = shape.index(max(shape))
    place[longest] = (place[longest] + 1) % shape[longest]
    return drawn.at[tuple(place)].set(high)


def steps_of(key, shape, pieces, low, top_value):
    def one(axis_at, blocks):
        heights = jax.random.uniform(jax.random.fold_in(jax.random.fold_in(key, 6), axis_at), (blocks,), jnp.float32, low / len(pieces), top_value / len(pieces))
        return jnp.repeat(jnp.exp(heights), shape[axis_at] // blocks).reshape((-1,) + (1,) * (len(shape) - axis_at - 1))

    level = one(*pieces[0])
    for cut in pieces[1:]:
        level = level * one(*cut)
    return level


def centred(key, shape, width, reach, cuts=(), kind=jnp.bfloat16):
    values = jax.random.normal(key, shape, jnp.float32) * width
    if len(cuts) > 0:
        values = steps_of(key, shape, cuts, -0.22, 0.18) * values
    return jnp.clip(values, min=-reach, max=reach).astype(kind)


def setup_inputs(seed: int = 0) -> dict:
    key_list = jax.random.split(jax.random.key(seed), 8)
    trans_real = jnp.clip(1.0 + 0.08 * jax.random.normal(key_list[0], (SLICES, N_TILE * PATCH, PATCH), jnp.float32), 0.6, 1.4)
    trans_imag = centred(key_list[1], (SLICES, N_TILE * PATCH, PATCH), 0.3, 1.5, ((0, 8), (1, 64)), jnp.float32)
    probe_real = centred(key_list[2], (WIN, WIN), 1.0, 6.0)
    probe_imag = centred(key_list[3], (WIN, WIN), 1.0, 6.0)
    offsets = set_ends(jax.random.randint(key_list[4], (2, POSITIONS), 0, PATCH - WIN + 1), jax.random.fold_in(key_list[4], 1), 0, PATCH - WIN).astype(jnp.int32)
    pattern_index = draw_pattern_index(jax.random.fold_in(key_list[7], 71), 0)
    measured = jnp.clip(jnp.exp(math.log(3.0) - 2.7119641 * jax.random.uniform(key_list[6], (POSITIONS, WIN, WIN), jnp.float32) ** steps_of(key_list[6], (POSITIONS, WIN, WIN), ((0, 64),), -0.2, 0.2)), 0.19921875, 3.0).astype(jnp.bfloat16)
    return {"trans_real": trans_real, "trans_imag": trans_imag, "probe_real": probe_real, "probe_imag": probe_imag, "offsets": offsets, "pattern_index": pattern_index, "measured": measured}


fresnel_strength = 9.0
softening = 0.01

def tables(extent):
    indices = jnp.arange(extent, dtype=jnp.int32)
    products = indices[:, None] * indices[None, :] % extent
    angles = products.astype(jnp.float32) * (2.0 * math.pi / extent)
    cosine = jnp.cos(angles)
    sines = jnp.sin(angles)
    frequency = jnp.where(indices < (extent + 1) // 2, indices, indices - extent).astype(jnp.float32) / extent
    phases = -fresnel_strength * frequency * frequency
    kernel_real = jnp.cos(phases)
    kernel_imag = jnp.sin(phases)
    scaled_real = cosine * kernel_real[None, :] - sines * kernel_imag[None, :]
    scaled_imag = cosine * kernel_imag[None, :] + sines * kernel_real[None, :]
    highest = lax.Precision.HIGHEST
    prop_real = (jnp.dot(scaled_real, cosine, precision=highest) + jnp.dot(scaled_imag, sines, precision=highest)) / extent
    prop_imag = (jnp.dot(scaled_imag, cosine, precision=highest) - jnp.dot(scaled_real, sines, precision=highest)) / extent
    norming = 1.0 / math.sqrt(extent)
    return (prop_real.astype(jnp.bfloat16), prop_imag.astype(jnp.bfloat16), (cosine * norming).astype(jnp.bfloat16), (-sines * norming).astype(jnp.bfloat16))

def left_product(matrix, field):
    return jnp.einsum('ab,nbc->nac', matrix.astype(jnp.float32), field.astype(jnp.float32))

def right_product(field, matrix):
    return jnp.einsum('nab,bc->nac', field.astype(jnp.float32), matrix.astype(jnp.float32))

def apply_both(mat_real, mat_imag, field_real, field_imag):
    mid_real = (left_product(mat_real, field_real) - left_product(mat_imag, field_imag)).astype(jnp.bfloat16)
    mid_imag = (left_product(mat_real, field_imag) + left_product(mat_imag, field_real)).astype(jnp.bfloat16)
    end_real = right_product(mid_real, mat_real) - right_product(mid_imag, mat_imag)
    end_imag = right_product(mid_real, mat_imag) + right_product(mid_imag, mat_real)
    return (end_real, end_imag)

def windows(patch_grid, offset_sel, extent):

    def cut_one(row_at, col_at):
        return lax.dynamic_slice(patch_grid, (row_at, col_at), (extent, extent))
    return jax.vmap(cut_one)(offset_sel[0], offset_sel[1])

def accumulate(patch_grid, contrib, offset_sel, extent):

    def add_one(item, acc):
        row_at = offset_sel[0, item]
        col_at = offset_sel[1, item]
        current = lax.dynamic_slice(acc, (row_at, col_at), (extent, extent))
        return lax.dynamic_update_slice(acc, current + contrib[item], (row_at, col_at))
    return lax.fori_loop(0, contrib.shape[0], add_one, patch_grid)

def forward_slice(win_real, win_imag, wave_real, wave_imag, prop_real, prop_imag):
    field_real = (win_real * wave_real.astype(jnp.float32) - win_imag * wave_imag.astype(jnp.float32)).astype(jnp.bfloat16)
    field_imag = (win_real * wave_imag.astype(jnp.float32) + win_imag * wave_real.astype(jnp.float32)).astype(jnp.bfloat16)
    out_real, out_imag = apply_both(prop_real, prop_imag, field_real, field_imag)
    return (out_real.astype(jnp.bfloat16), out_imag.astype(jnp.bfloat16))

def modulus(exit_real, exit_imag, amplitude, four_real, four_imag):
    far_real, far_imag = apply_both(four_real, four_imag, exit_real, exit_imag)
    amp = jnp.sqrt(far_real * far_real + far_imag * far_imag + softening)
    ratio = (amp - amplitude.astype(jnp.float32)) / amp
    resid_real = (ratio * far_real).astype(jnp.bfloat16)
    resid_imag = (ratio * far_imag).astype(jnp.bfloat16)
    back_real, back_imag = apply_both(four_real, -four_imag, resid_real, resid_imag)
    return (back_real.astype(jnp.bfloat16), back_imag.astype(jnp.bfloat16))

def backward_slice(win_real, win_imag, grad_real, grad_imag, wave_real, wave_imag, prop_real, prop_imag):
    back_real, back_imag = apply_both(prop_real, -prop_imag, grad_real, grad_imag)
    psi_real = wave_real.astype(jnp.float32)
    psi_imag = wave_imag.astype(jnp.float32)
    contrib_real = back_real * psi_real + back_imag * psi_imag
    contrib_imag = back_imag * psi_real - back_real * psi_imag
    out_real = (back_real * win_real + back_imag * win_imag).astype(jnp.bfloat16)
    out_imag = (back_imag * win_real - back_real * win_imag).astype(jnp.bfloat16)
    return (contrib_real, contrib_imag, out_real, out_imag)

def reference(trans_real, trans_imag, probe_real, probe_imag, offsets, pattern_index, measured):
    prop_real, prop_imag, four_real, four_imag = tables(WIN)

    def one_tile(tile_no):
        first = (tile_no * POS_TILE).astype(jnp.int32)
        offset_sel = lax.dynamic_slice_in_dim(offsets, first, POS_TILE, 1)
        rows_sel = lax.dynamic_slice_in_dim(pattern_index, first, POS_TILE, 0)
        amplitude = jnp.take(measured, rows_sel, axis=0)
        corner = (tile_no * PATCH).astype(jnp.int32)
        patch_real = lax.dynamic_slice_in_dim(trans_real, corner, PATCH, 1)
        patch_imag = lax.dynamic_slice_in_dim(trans_imag, corner, PATCH, 1)
        wave_real = jnp.broadcast_to(probe_real, (POS_TILE, WIN, WIN))
        wave_imag = jnp.broadcast_to(probe_imag, (POS_TILE, WIN, WIN))
        stored = []
        for layer in range(SLICES):
            win_real = windows(patch_real[layer], offset_sel, WIN)
            win_imag = windows(patch_imag[layer], offset_sel, WIN)
            stored.append((wave_real, wave_imag))
            wave_real, wave_imag = forward_slice(win_real, win_imag, wave_real, wave_imag, prop_real, prop_imag)
        grad_real, grad_imag = modulus(wave_real, wave_imag, amplitude, four_real, four_imag)
        real_parts = [None] * SLICES
        imag_parts = [None] * SLICES
        for layer in reversed(range(SLICES)):
            win_real = windows(patch_real[layer], offset_sel, WIN)
            win_imag = windows(patch_imag[layer], offset_sel, WIN)
            contrib_real, contrib_imag, grad_real, grad_imag = backward_slice(win_real, win_imag, grad_real, grad_imag, stored[layer][0], stored[layer][1], prop_real, prop_imag)
            empty = jnp.zeros((PATCH, PATCH), jnp.float32)
            real_parts[layer] = accumulate(empty, contrib_real, offset_sel, WIN)
            imag_parts[layer] = accumulate(empty, contrib_imag, offset_sel, WIN)
        return jnp.stack([jnp.stack(real_parts), jnp.stack(imag_parts)])
    tile_ids = jnp.arange(N_TILE, dtype=jnp.int32)
    result = lax.map(one_tile, tile_ids)
    return jnp.transpose(result, (1, 2, 0, 3, 4)).reshape(2, SLICES, N_TILE * PATCH, PATCH)
```

```python
import math

import jax
import jax.numpy as jnp
import ml_dtypes
import numpy as np
from jax import lax
from jax.experimental import pallas as pl
from jax.experimental.pallas import tpu as pltpu
from jax.sharding import PartitionSpec as P

fresnel_strength = 9.0
softening = 0.01

CODE_TOP = 32766.0
REAL_MID = 1.0
REAL_HALF = 0.4
IMAG_HALF = 1.5


def tables(extent):
    indices = np.arange(extent)
    angles = (indices[:, None] * indices[None, :] % extent) * (2.0 * math.pi / extent)
    whole = np.cos(angles) + 1j * np.sin(angles)
    frequency = np.where(indices < (extent + 1) // 2, indices, indices - extent) / extent
    prop = (whole * np.exp(-1j * fresnel_strength * frequency**2)[None, :]) @ whole.conj() / extent
    four = whole.conj() / math.sqrt(extent)
    blocks = []
    for matrix in (prop, four):
        real = matrix.real.astype(np.float32).astype(ml_dtypes.bfloat16)
        imag = matrix.imag.astype(np.float32).astype(ml_dtypes.bfloat16)
        blocks.append(np.block([[real, -imag], [imag, real]]))
        blocks.append(np.block([[real, imag], [-imag, real]]))
    return np.stack(blocks).astype(ml_dtypes.bfloat16)


def encode(trans_real, trans_imag):
    real = jnp.round((trans_real - REAL_MID) * (CODE_TOP / REAL_HALF)).astype(jnp.int32)
    imag = jnp.round(trans_imag * (CODE_TOP / IMAG_HALF)).astype(jnp.int32)
    return (real << 16) | (imag & 0xFFFF)


def decode(code):
    real = (code >> 16).astype(jnp.float32) * (REAL_HALF / CODE_TOP) + REAL_MID
    imag = ((code << 16) >> 16).astype(jnp.float32) * (IMAG_HALF / CODE_TOP)
    return real, imag


def quarters(square):
    half = square.shape[0] // 2
    return (square[:half, :half], square[:half, half:], square[half:, :half], square[half:, half:])


def joined(a, b, c, d):
    return jnp.concatenate(
        [jnp.concatenate([a, b], axis=1), jnp.concatenate([c, d], axis=1)], axis=0
    )


def both_sides(left, right, field):
    real0, imag0, real1, imag1 = quarters(field)
    mid = jnp.dot(
        left, joined(real0, real1, imag0, imag1), preferred_element_type=jnp.float32
    ).astype(jnp.bfloat16)
    real0, real1, imag0, imag1 = quarters(mid)
    return jnp.dot(
        joined(real0, imag0, real1, imag1), right, preferred_element_type=jnp.float32
    )


def gradient_kernel(
    offset_ref, patch_ref, probe_ref, amp_ref, table_ref, out_ref, code_ref, wave_ref, grad_ref, sum_ref
):
    slices, side, _ = patch_ref.shape
    extent = probe_ref.shape[1]
    count = code_ref.shape[1]
    pairs = count // 2
    pieces, _, piece_rows, _ = amp_ref.shape

    tall = extent + 8

    def placed(position):
        row_at = offset_ref[0, position]
        start = jnp.minimum(row_at // 8, (side - tall) // 8) * 8
        return pl.multiple_of(start, 8), row_at - start

    def part(pair, item):
        return pair * 2 + item, slice(item * extent, (item + 1) * extent)

    for pair in range(pairs):
        for item in range(2):
            _, rows = part(pair, item)
            wave_ref[0, pair, rows, :extent] = probe_ref[0]
            wave_ref[0, pair, rows, extent:] = probe_ref[1]

    def descend(layer, carry):
        for pair in range(pairs):
            fields = []
            for item in range(2):
                position, rows = part(pair, item)
                row_at, down = placed(position)
                back = lax.rem(side - offset_ref[1, position], side)
                code = pltpu.roll(patch_ref[layer, pl.ds(row_at, tall), :], back, 1)[:, :extent]
                code = pltpu.roll(code, lax.rem(tall - down, tall), 0)[:extent]
                code_ref[layer, position] = code
                t_real, t_imag = decode(code)
                wave = wave_ref[layer, pair, rows, :].astype(jnp.float32)
                w_real, w_imag = wave[:, :extent], wave[:, extent:]
                fields.append(
                    jnp.concatenate(
                        [t_real * w_real - t_imag * w_imag, t_real * w_imag + t_imag * w_real], axis=1
                    ).astype(jnp.bfloat16)
                )
            ahead = both_sides(table_ref[0], table_ref[1], jnp.concatenate(fields, axis=0))
            wave_ref[layer + 1, pair] = ahead.astype(jnp.bfloat16)
        return carry

    lax.fori_loop(0, slices, descend, 0)

    for pair in range(pairs):
        far = both_sides(table_ref[2], table_ref[3], wave_ref[slices, pair])
        residue = []
        for item in range(2):
            position, rows = part(pair, item)
            f_real, f_imag = far[rows, :extent], far[rows, extent:]
            amplitude = jnp.concatenate(
                [amp_ref[piece, position] for piece in range(pieces)], axis=0
            ).astype(jnp.float32)
            amp = jnp.sqrt(f_real * f_real + f_imag * f_imag + softening)
            ratio = (amp - amplitude) / amp
            residue.append(
                jnp.concatenate([ratio * f_real, ratio * f_imag], axis=1).astype(jnp.bfloat16)
            )
        back = both_sides(table_ref[3], table_ref[2], jnp.concatenate(residue, axis=0))
        grad_ref[pair] = back.astype(jnp.bfloat16)

    def ascend(step, carry):
        layer = slices - 1 - step
        sum_ref[...] = jnp.zeros_like(sum_ref)
        for pair in range(pairs):
            back = both_sides(table_ref[1], table_ref[0], grad_ref[pair])
            for item in range(2):
                position, rows = part(pair, item)
                u_real, u_imag = back[rows, :extent], back[rows, extent:]
                t_real, t_imag = decode(code_ref[layer, position])
                grad_ref[pair, rows, :extent] = (u_real * t_real + u_imag * t_imag).astype(jnp.bfloat16)
                grad_ref[pair, rows, extent:] = (u_imag * t_real - u_real * t_imag).astype(jnp.bfloat16)
                wave = wave_ref[layer, pair, rows, :].astype(jnp.float32)
                w_real, w_imag = wave[:, :extent], wave[:, extent:]
                row_at, down = placed(position)
                col_at = offset_ref[1, position]
                for plane, contrib in enumerate(
                    (u_real * w_real + u_imag * w_imag, u_imag * w_real - u_real * w_imag)
                ):
                    high = jnp.concatenate(
                        [contrib, jnp.zeros((tall - extent, extent), jnp.float32)], axis=0
                    )
                    wide = jnp.concatenate(
                        [pltpu.roll(high, down, 0), jnp.zeros((tall, side - extent), jnp.float32)],
                        axis=1,
                    )
                    sum_ref[plane, pl.ds(row_at, tall), :] += pltpu.roll(wide, col_at, 1)
        out_ref[layer, :side] = sum_ref[0].astype(jnp.bfloat16)
        out_ref[layer, side:] = sum_ref[1].astype(jnp.bfloat16)
        return carry

    lax.fori_loop(0, slices, ascend, 0)


def patch_gradient(offset_mine, patches, probe, amp_pieces, table):
    slices, side, _ = patches.shape
    extent = probe.shape[-1]
    count = offset_mine.shape[1]
    vmem = pl.BlockSpec(memory_space=pltpu.VMEM)
    return pl.pallas_call(
        gradient_kernel,
        out_shape=jax.ShapeDtypeStruct((slices, 2 * side, side), jnp.bfloat16),
        in_specs=[pl.BlockSpec(memory_space=pltpu.SMEM), vmem, vmem, vmem, vmem],
        out_specs=vmem,
        scratch_shapes=[
            pltpu.VMEM((slices, count, extent, extent), jnp.int32),
            pltpu.VMEM((slices + 1, count // 2, 2 * extent, 2 * extent), jnp.bfloat16),
            pltpu.VMEM((count // 2, 2 * extent, 2 * extent), jnp.bfloat16),
            pltpu.VMEM((2, side, side), jnp.float32),
        ],
        name="patch_gradient",
        compiler_params=pltpu.CompilerParams(vmem_limit_bytes=40 << 20),
        cost_estimate=pl.CostEstimate(
            flops=2 * (slices + 1) * 2 * count * 8 * extent**3, bytes_accessed=6 << 20, transcendentals=0
        ),
    )(offset_mine, patches, probe, amp_pieces, table)


def fetch_patterns(pattern_index, measured, section_no, sections):
    positions = pattern_index.shape[0]
    tile_count = lax.axis_size("tile")
    extent = measured.shape[1]
    share = extent // sections
    owners = pattern_index // positions
    slots = pattern_index % positions
    named = owners[None, :] == jnp.arange(tile_count, dtype=jnp.int32)[:, None]
    request = jnp.sum(jnp.where(named, slots[None, :], 0), axis=1)
    requested = lax.all_to_all(request, "tile", split_axis=0, concat_axis=0, tiled=True)
    mine = lax.dynamic_slice_in_dim(measured, section_no * share, share, 1)
    answered = lax.all_to_all(
        jnp.take(mine, requested, axis=0), "tile", split_axis=0, concat_axis=0, tiled=True
    )
    return jnp.take(answered, owners, axis=0)


def local(trans_real, trans_imag, probe_real, probe_imag, offsets, pattern_index, measured):
    extent = probe_real.shape[-1]
    side = trans_real.shape[-1]
    positions = pattern_index.shape[0]
    sections = lax.axis_size("cuts")
    section_no = lax.axis_index("cuts")
    per_batch = positions // sections
    table = jnp.asarray(tables(extent))
    pieces = fetch_patterns(pattern_index, measured, section_no, sections)
    amp_pieces = lax.all_to_all(
        pieces.reshape(sections, per_batch, extent // sections, extent),
        "cuts",
        split_axis=0,
        concat_axis=0,
        tiled=True,
    )
    patches = lax.all_gather(encode(trans_real, trans_imag), "cuts", axis=0, tiled=True)
    offset_mine = lax.dynamic_slice_in_dim(offsets, section_no * per_batch, per_batch, 1)
    partial = patch_gradient(
        offset_mine, patches, jnp.stack([probe_real, probe_imag]), amp_pieces, table
    )
    parts = lax.all_to_all(partial, "cuts", split_axis=0, concat_axis=0, tiled=True)
    total = jnp.sum(parts.astype(jnp.float32), axis=0)
    return total.reshape(2, 1, side, side)


def solution(mesh):
    return jax.shard_map(
        local,
        mesh=mesh,
        in_specs=(
            P("cuts", "tile", None),
            P("cuts", "tile", None),
            P(),
            P(),
            P(None, "tile"),
            P("tile"),
            P("tile", None, None),
        ),
        out_specs=P(None, "cuts", "tile", None),
        check_vma=False,
    )
```

```python
import math

import jax
import jax.numpy as jnp
import ml_dtypes
import numpy as np
from jax import lax
from jax.experimental import pallas as pl
from jax.experimental.pallas import tpu as pltpu
from jax.sharding import PartitionSpec as P


fresnel_strength = 9.0
softening = 0.01

CODE_TOP = 32766.0
REAL_MID = 1.0
REAL_HALF = 0.4
IMAG_HALF = 1.5


def tables(extent):
    indices = np.arange(extent)
    angles = (indices[:, None] * indices[None, :] % extent) * (2.0 * math.pi / extent)
    whole = np.cos(angles) + 1j * np.sin(angles)
    frequency = np.where(indices < (extent + 1) // 2, indices, indices - extent) / extent
    prop = (whole * np.exp(-1j * fresnel_strength * frequency**2)[None, :]) @ whole.conj() / extent
    four = whole.conj() / math.sqrt(extent)
    blocks = []
    for matrix in (prop, four):
        real = matrix.real.astype(np.float32).astype(ml_dtypes.bfloat16)
        imag = matrix.imag.astype(np.float32).astype(ml_dtypes.bfloat16)
        blocks.append(np.block([[real, -imag], [imag, real]]))
        blocks.append(np.block([[real, imag], [-imag, real]]))
    return np.stack(blocks).astype(ml_dtypes.bfloat16)


def encode(trans_real, trans_imag):
    real = jnp.round((trans_real - REAL_MID) * (CODE_TOP / REAL_HALF)).astype(jnp.int32)
    imag = jnp.round(trans_imag * (CODE_TOP / IMAG_HALF)).astype(jnp.int32)
    return (real << 16) | (imag & 0xFFFF)


def decode(code):
    real = (code >> 16).astype(jnp.float32) * (REAL_HALF / CODE_TOP) + REAL_MID
    imag = ((code << 16) >> 16).astype(jnp.float32) * (IMAG_HALF / CODE_TOP)
    return real, imag


def quarters(square):
    half = square.shape[0] // 2
    return (square[:half, :half], square[:half, half:], square[half:, :half], square[half:, half:])


def joined(a, b, c, d):
    return jnp.concatenate(
        [jnp.concatenate([a, b], axis=1), jnp.concatenate([c, d], axis=1)], axis=0
    )


def both_sides(left, right, field):
    real0, imag0, real1, imag1 = quarters(field)
    mid = jnp.dot(
        left, joined(real0, real1, imag0, imag1), preferred_element_type=jnp.float32
    ).astype(jnp.bfloat16)
    real0, real1, imag0, imag1 = quarters(mid)
    return jnp.dot(
        joined(real0, imag0, real1, imag1), right, preferred_element_type=jnp.float32
    )


def placed(offset_ref, position, side, tall):
    row_at = offset_ref[0, position]
    start = jnp.minimum(row_at // 8, (side - tall) // 8) * 8
    return pl.multiple_of(start, 8), row_at - start


def part(extent, pair, item):
    return pair * 2 + item, slice(item * extent, (item + 1) * extent)


def descend_kernel(
    offset_ref, order_ref, table_hbm, probe_ref, *refs
):
    patches_hbm = refs[:-12]
    codes_hbm, waves_hbm, far_hbm = refs[-12:-9]
    table_ref, patch_ref, code_ref, wave_ref, far_ref, table_sem, patch_sem, code_sem, wave_sem = refs[-9:]
    slices, count, extent, _ = code_ref.shape
    side = patch_ref.shape[-1]
    pairs = count // 2
    tall = extent + 8

    table_in = pltpu.make_async_copy(table_hbm, table_ref, table_sem)
    table_in.start()
    for place, hbm in enumerate(patches_hbm):
        layer = order_ref[place]
        pltpu.make_async_copy(hbm.at[0], patch_ref.at[layer], patch_sem.at[layer]).start()
    for pair in range(pairs):
        for item in range(2):
            _, rows = part(extent, pair, item)
            wave_ref[0, pair, rows, :extent] = probe_ref[0]
            wave_ref[0, pair, rows, extent:] = probe_ref[1]
    table_in.wait()

    def code_out(layer):
        return pltpu.make_async_copy(code_ref.at[layer], codes_hbm.at[layer], code_sem.at[layer])

    def wave_out(layer):
        return pltpu.make_async_copy(wave_ref.at[layer], waves_hbm.at[layer - 1], wave_sem.at[layer])

    def descend(layer, carry):
        pltpu.make_async_copy(patches_hbm[0].at[0], patch_ref.at[layer], patch_sem.at[layer]).wait()
        for pair in range(pairs):
            fields = []
            for item in range(2):
                position, rows = part(extent, pair, item)
                row_at, down = placed(offset_ref, position, side, tall)
                back = lax.rem(side - offset_ref[1, position], side)
                code = pltpu.roll(patch_ref[layer, pl.ds(row_at, tall), :], back, 1)[:, :extent]
                code = pltpu.roll(code, lax.rem(tall - down, tall), 0)[:extent]
                code_ref[layer, position] = code
                t_real, t_imag = decode(code)
                wave = wave_ref[layer, pair, rows, :].astype(jnp.float32)
                w_real, w_imag = wave[:, :extent], wave[:, extent:]
                fields.append(
                    jnp.concatenate(
                        [t_real * w_real - t_imag * w_imag, t_real * w_imag + t_imag * w_real], axis=1
                    ).astype(jnp.bfloat16)
                )
            ahead = both_sides(table_ref[0], table_ref[1], jnp.concatenate(fields, axis=0))
            wave_ref[layer + 1, pair] = ahead.astype(jnp.bfloat16)
        code_out(layer).start()

        @pl.when(layer < slices - 1)
        def _():
            wave_out(layer + 1).start()

        return carry

    lax.fori_loop(0, slices, descend, 0)
    for pair in range(pairs):
        far_ref[pair] = both_sides(table_ref[2], table_ref[3], wave_ref[slices, pair])
    far_out = pltpu.make_async_copy(far_ref, far_hbm, table_sem)
    far_out.start()
    for layer in range(slices):
        code_out(layer).wait()
        if layer > 0:
            wave_out(layer).wait()
    far_out.wait()


def ascend_kernel(
    offset_ref,
    core_ref,
    table_hbm,
    probe_ref,
    amp_ref,
    codes_hbm,
    waves_hbm,
    far_hbm,
    own_ref,
    other_ref,
    table_ref,
    code_ref,
    wave_ref,
    far_ref,
    grad_ref,
    sum_ref,
    table_sem,
    far_sem,
    code_sem,
    wave_sem,
):
    slices, count, extent, _ = code_ref.shape
    side = own_ref.shape[-1]
    pairs = count // 2
    pieces = amp_ref.shape[0]
    tall = extent + 8

    far_in = pltpu.make_async_copy(far_hbm, far_ref, far_sem)
    far_in.start()
    table_in = pltpu.make_async_copy(table_hbm, table_ref, table_sem)
    table_in.start()

    def code_in(layer):
        return pltpu.make_async_copy(codes_hbm.at[layer], code_ref.at[layer], code_sem.at[layer])

    def wave_in(layer):
        return pltpu.make_async_copy(waves_hbm.at[layer - 1], wave_ref.at[layer], wave_sem.at[layer])

    for layer in reversed(range(slices)):
        code_in(layer).start()
        if layer > 0:
            wave_in(layer).start()
    for pair in range(pairs):
        for item in range(2):
            _, rows = part(extent, pair, item)
            wave_ref[0, pair, rows, :extent] = probe_ref[0]
            wave_ref[0, pair, rows, extent:] = probe_ref[1]
    far_in.wait()
    table_in.wait()

    for pair in range(pairs):
        residue = []
        for item in range(2):
            position, rows = part(extent, pair, item)
            f_real, f_imag = far_ref[pair, rows, :extent], far_ref[pair, rows, extent:]
            amplitude = jnp.concatenate(
                [amp_ref[piece, position] for piece in range(pieces)], axis=0
            ).astype(jnp.float32)
            amp = jnp.sqrt(f_real * f_real + f_imag * f_imag + softening)
            ratio = (amp - amplitude) / amp
            residue.append(
                jnp.concatenate([ratio * f_real, ratio * f_imag], axis=1).astype(jnp.bfloat16)
            )
        back = both_sides(table_ref[3], table_ref[2], jnp.concatenate(residue, axis=0))
        grad_ref[pair] = back.astype(jnp.bfloat16)

    def ascend(step, carry):
        layer = slices - 1 - step
        code_in(layer).wait()

        @pl.when(layer > 0)
        def _():
            wave_in(layer).wait()

        sum_ref[...] = jnp.zeros_like(sum_ref)
        for pair in range(pairs):
            back = both_sides(table_ref[1], table_ref[0], grad_ref[pair])
            for item in range(2):
                position, rows = part(extent, pair, item)
                u_real, u_imag = back[rows, :extent], back[rows, extent:]
                t_real, t_imag = decode(code_ref[layer, position])
                grad_ref[pair, rows, :extent] = (u_real * t_real + u_imag * t_imag).astype(jnp.bfloat16)
                grad_ref[pair, rows, extent:] = (u_imag * t_real - u_real * t_imag).astype(jnp.bfloat16)
                wave = wave_ref[layer, pair, rows, :].astype(jnp.float32)
                w_real, w_imag = wave[:, :extent], wave[:, extent:]
                row_at, down = placed(offset_ref, position, side, tall)
                col_at = offset_ref[1, position]
                for plane, contrib in enumerate(
                    (u_real * w_real + u_imag * w_imag, u_imag * w_real - u_real * w_imag)
                ):
                    high = jnp.concatenate(
                        [contrib, jnp.zeros((tall - extent, extent), jnp.float32)], axis=0
                    )
                    wide = jnp.concatenate(
                        [pltpu.roll(high, down, 0), jnp.zeros((tall, side - extent), jnp.float32)],
                        axis=1,
                    )
                    sum_ref[plane, pl.ds(row_at, tall), :] += pltpu.roll(wide, col_at, 1)
        mine = layer % 2 == core_ref[0]

        @pl.when(mine)
        def _():
            own_ref[layer // 2, :side] = sum_ref[0].astype(jnp.bfloat16)
            own_ref[layer // 2, side:] = sum_ref[1].astype(jnp.bfloat16)

        @pl.when(jnp.logical_not(mine))
        def _():
            other_ref[layer // 2, :side] = sum_ref[0].astype(jnp.bfloat16)
            other_ref[layer // 2, side:] = sum_ref[1].astype(jnp.bfloat16)

        return carry

    lax.fori_loop(0, slices, ascend, 0)


SMEM = pl.BlockSpec(memory_space=pltpu.SMEM)
VMEM = pl.BlockSpec(memory_space=pltpu.VMEM)
HBM = pl.BlockSpec(memory_space=pltpu.HBM)
FULL = 67_043_328
PARAMS = pltpu.CompilerParams(vmem_limit_bytes=FULL - (1 << 19))


def forward(offset_mine, order, patches, probe, table):
    slices = len(patches)
    side = patches[0].shape[-1]
    extent = probe.shape[-1]
    count = offset_mine.shape[1]
    square = (count // 2, 2 * extent, 2 * extent)
    return pl.pallas_call(
        descend_kernel,
        out_shape=(
            jax.ShapeDtypeStruct((slices, count, extent, extent), jnp.int32),
            jax.ShapeDtypeStruct((slices - 1,) + square, jnp.bfloat16),
            jax.ShapeDtypeStruct(square, jnp.float32),
        ),
        in_specs=[SMEM, SMEM, HBM, VMEM] + [HBM] * slices,
        out_specs=(HBM, HBM, HBM),
        scratch_shapes=[
            pltpu.VMEM(table.shape, table.dtype),
            pltpu.VMEM((slices, side, side), jnp.int32),
            pltpu.VMEM((slices, count, extent, extent), jnp.int32),
            pltpu.VMEM((slices + 1,) + square, jnp.bfloat16),
            pltpu.VMEM(square, jnp.float32),
            pltpu.SemaphoreType.DMA,
            pltpu.SemaphoreType.DMA((slices,)),
            pltpu.SemaphoreType.DMA((slices,)),
            pltpu.SemaphoreType.DMA((slices,)),
        ],
        name="descend",
        compiler_params=PARAMS,
        cost_estimate=pl.CostEstimate(
            flops=2 * (slices + 1) * count * 8 * extent**3, bytes_accessed=6 << 20, transcendentals=0
        ),
    )(offset_mine, order, table, probe, *patches)


def backward(offset_mine, core, table, probe, amp_pieces, codes, waves, far, side):
    slices, count, extent, _ = codes.shape
    half = jax.ShapeDtypeStruct((slices // 2, 2 * side, side), jnp.bfloat16)
    square = (count // 2, 2 * extent, 2 * extent)
    return pl.pallas_call(
        ascend_kernel,
        out_shape=(half, half),
        in_specs=[SMEM, SMEM, HBM, VMEM, VMEM, HBM, HBM, HBM],
        out_specs=(VMEM, VMEM),
        scratch_shapes=[
            pltpu.VMEM(table.shape, table.dtype),
            pltpu.VMEM((slices, count, extent, extent), jnp.int32),
            pltpu.VMEM((slices,) + square, jnp.bfloat16),
            pltpu.VMEM(square, jnp.float32),
            pltpu.VMEM(square, jnp.bfloat16),
            pltpu.VMEM((2, side, side), jnp.float32),
            pltpu.SemaphoreType.DMA,
            pltpu.SemaphoreType.DMA,
            pltpu.SemaphoreType.DMA((slices,)),
            pltpu.SemaphoreType.DMA((slices,)),
        ],
        name="ascend",
        compiler_params=pltpu.CompilerParams(vmem_limit_bytes=FULL - (5 << 19)),
        cost_estimate=pl.CostEstimate(
            flops=2 * (slices + 1) * count * 8 * extent**3, bytes_accessed=6 << 20, transcendentals=0
        ),
    )(offset_mine, core, table, probe, amp_pieces, codes, waves, far)


def fetch_patterns(pattern_index, measured, section_no, sections):
    positions, extent, _ = measured.shape
    tile_count = lax.axis_size("tile")
    share = extent // sections
    owners = pattern_index // positions
    slots = pattern_index % positions
    named = owners[None, :] == jnp.arange(tile_count, dtype=jnp.int32)[:, None]
    request = jnp.sum(jnp.where(named, slots[None, :], 0), axis=1)
    requested = lax.all_to_all(request, "tile", split_axis=0, concat_axis=0, tiled=True)
    mine = lax.dynamic_slice_in_dim(measured, section_no * share, share, 1)
    rows = mine.at[requested].get(mode="promise_in_bounds")
    answered = lax.all_to_all(rows, "tile", split_axis=0, concat_axis=0, tiled=True)
    pieces = answered.at[owners].get(mode="promise_in_bounds")
    pieces = pieces.reshape(sections, positions // sections, share, extent)
    return lax.all_to_all(pieces, "cuts", split_axis=0, concat_axis=0, tiled=True)


def across(chips, step):
    return [(2 * at + core, 2 * ((at + step) % chips) + core) for at in range(chips) for core in range(2)]


def local(trans_real, trans_imag, probe_real, probe_imag, offsets, pattern_index, measured):
    extent = probe_real.shape[-1]
    side = trans_real.shape[-1]
    positions = pattern_index.shape[0]
    sections = lax.axis_size("cuts")
    section_no = lax.axis_index("cuts")
    per_batch = positions // sections
    chips = sections // 2
    chip, core = section_no // 2, section_no % 2
    sibling = [(at, at ^ 1) for at in range(sections)]
    steps = sorted(range(1, chips), key=lambda step: min(step, chips - step))

    table = jnp.asarray(tables(extent))
    probe = jnp.stack([probe_real, probe_imag])
    offset_mine = lax.dynamic_slice_in_dim(offsets, section_no * per_batch, per_batch, 1)
    amp_pieces = fetch_patterns(pattern_index, measured, section_no, sections)
    code = encode(trans_real, trans_imag)
    patches = [code] + [lax.ppermute(code, "cuts", across(chips, step)) for step in steps]
    near = [lax.ppermute(code, "cuts", sibling)]
    near += [lax.ppermute(patch, "cuts", sibling) for patch in patches[1:]]
    came = (chip - jnp.array([0] + steps, jnp.int32)) % chips * 2
    order = jnp.concatenate([came + core, came + 1 - core])
    codes, waves, far = forward(offset_mine, order, patches + near, probe, table)
    own, other = backward(
        offset_mine, core[None], table, probe, amp_pieces, codes, waves, far, side
    )
    met = lax.ppermute(other, "cuts", sibling)
    paired = (own.astype(jnp.float32) + met.astype(jnp.float32)).astype(jnp.bfloat16)
    groups = [[2 * at + parity for at in range(chips)] for parity in range(2)]
    parts = lax.all_to_all(
        paired, "cuts", split_axis=0, concat_axis=0, tiled=True, axis_index_groups=groups
    )
    total = jnp.sum(parts.astype(jnp.float32), axis=0)
    return total.reshape(2, 1, side, side)


def solution(mesh):
    return jax.shard_map(
        local,
        mesh=mesh,
        in_specs=(
            P("cuts", "tile", None),
            P("cuts", "tile", None),
            P(),
            P(),
            P(None, "tile"),
            P("tile"),
            P("tile", None, None),
        ),
        out_specs=P(None, "cuts", "tile", None),
        check_vma=False,
    )
```

```python
import functools
import math

import jax
import jax.numpy as jnp
import ml_dtypes
import numpy as np
from jax import lax
from jax.experimental import pallas as pl
from jax.experimental.pallas import tpu as pltpu
from jax.sharding import PartitionSpec as P


fresnel_strength = 9.0
softening = 0.01

CODE_TOP = 32766.0
REAL_MID = 1.0
REAL_HALF = 0.4
IMAG_HALF = 1.5


def tables(extent):
    indices = np.arange(extent)
    angles = (indices[:, None] * indices[None, :] % extent) * (2.0 * math.pi / extent)
    whole = np.cos(angles) + 1j * np.sin(angles)
    frequency = np.where(indices < (extent + 1) // 2, indices, indices - extent) / extent
    prop = (whole * np.exp(-1j * fresnel_strength * frequency**2)[None, :]) @ whole.conj() / extent
    four = whole.conj() / math.sqrt(extent)
    blocks = []
    for matrix in (prop, four):
        real = matrix.real.astype(np.float32).astype(ml_dtypes.bfloat16)
        imag = matrix.imag.astype(np.float32).astype(ml_dtypes.bfloat16)
        blocks.append(np.block([[real, -imag], [imag, real]]))
        blocks.append(np.block([[real, imag], [-imag, real]]))
    return np.stack(blocks).astype(ml_dtypes.bfloat16)


def encode(trans_real, trans_imag):
    real = jnp.round((trans_real - REAL_MID) * (CODE_TOP / REAL_HALF)).astype(jnp.int32)
    imag = jnp.round(trans_imag * (CODE_TOP / IMAG_HALF)).astype(jnp.int32)
    return (real << 16) | (imag & 0xFFFF)


def decode(code):
    real = (code >> 16).astype(jnp.float32) * (REAL_HALF / CODE_TOP) + REAL_MID
    imag = ((code << 16) >> 16).astype(jnp.float32) * (IMAG_HALF / CODE_TOP)
    return real, imag


def quarters(square):
    half = square.shape[0] // 2
    return (square[:half, :half], square[:half, half:], square[half:, :half], square[half:, half:])


def joined(a, b, c, d):
    return jnp.concatenate(
        [jnp.concatenate([a, b], axis=1), jnp.concatenate([c, d], axis=1)], axis=0
    )


def both_sides(left, right, field):
    real0, imag0, real1, imag1 = quarters(field)
    mid = jnp.dot(
        left, joined(real0, real1, imag0, imag1), preferred_element_type=jnp.float32
    ).astype(jnp.bfloat16)
    real0, real1, imag0, imag1 = quarters(mid)
    return jnp.dot(
        joined(real0, imag0, real1, imag1), right, preferred_element_type=jnp.float32
    )


def placed(offset_ref, position, side, tall):
    mine = lax.axis_index("cuts") * (offset_ref.shape[1] // lax.axis_size("cuts")) + position
    row_at = offset_ref[0, mine]
    start = jnp.minimum(row_at // 8, (side - tall) // 8) * 8
    return offset_ref[1, mine], pl.multiple_of(start, 8), row_at - start


def part(extent, pair, item):
    return pair * 2 + item, slice(item * extent, (item + 1) * extent)


def ask_kernel(index_ref, request_ref, *, stored):
    request_ref[...] = jnp.zeros_like(request_ref)
    for position in range(index_ref.shape[0]):
        index = index_ref[position]
        slot = jnp.full(request_ref.shape[1:], lax.rem(index, stored), request_ref.dtype)
        request_ref[lax.div(index, stored)] = slot


def pick_kernel(wanted_ref, shares_ref, rows_ref):
    for tile in range(rows_ref.shape[0]):
        rows_ref[tile] = shares_ref[wanted_ref[tile, 0, 0]]


def sort_kernel(index_ref, answered_ref, rows_ref, *, stored):
    for position in range(rows_ref.shape[0]):
        rows_ref[position] = answered_ref[lax.div(index_ref[position], stored)]


def descend_kernel(
    offset_ref,
    mine_hbm,
    theirs_hbm,
    table_hbm,
    probe_real_ref,
    probe_imag_ref,
    codes_hbm,
    wave_ref,
    table_ref,
    patch_ref,
    code_ref,
    table_sem,
    patch_sem,
    code_sem,
    *,
    steps,
):
    slices, count, extent, _ = code_ref.shape
    side = patch_ref.shape[-1]
    pairs = count // 2
    tall = extent + 8
    chips = len(steps)
    section_no = lax.axis_index("cuts")
    chip, core = section_no // 2, section_no % 2

    table_in = pltpu.make_async_copy(table_hbm.at[pl.ds(0, 2)], table_ref, table_sem)
    table_in.start()
    for place, step in enumerate(steps):
        came = (chip + chips - step) % chips * 2
        for hbm, layer in ((mine_hbm, came + core), (theirs_hbm, came + 1 - core)):
            pltpu.make_async_copy(hbm.at[place], patch_ref.at[layer], patch_sem.at[layer]).start()
    for pair in range(pairs):
        for item in range(2):
            _, rows = part(extent, pair, item)
            wave_ref[0, pair, rows, :extent] = probe_real_ref[...]
            wave_ref[0, pair, rows, extent:] = probe_imag_ref[...]
    table_in.wait()

    def code_out(layer):
        return pltpu.make_async_copy(code_ref.at[layer], codes_hbm.at[layer], code_sem.at[layer])

    def descend(layer, carry):
        pltpu.make_async_copy(mine_hbm.at[0], patch_ref.at[layer], patch_sem.at[layer]).wait()
        for pair in range(pairs):
            fields = []
            for item in range(2):
                position, rows = part(extent, pair, item)
                col_at, row_at, down = placed(offset_ref, position, side, tall)
                back = lax.rem(side - col_at, side)
                code = pltpu.roll(patch_ref[layer, pl.ds(row_at, tall), :], back, 1)[:, :extent]
                code = pltpu.roll(code, lax.rem(tall - down, tall), 0)[:extent]
                code_ref[layer, position] = code
                t_real, t_imag = decode(code)
                wave = wave_ref[layer, pair, rows, :].astype(jnp.float32)
                w_real, w_imag = wave[:, :extent], wave[:, extent:]
                fields.append(
                    jnp.concatenate(
                        [t_real * w_real - t_imag * w_imag, t_real * w_imag + t_imag * w_real], axis=1
                    ).astype(jnp.bfloat16)
                )
            ahead = both_sides(table_ref[0], table_ref[1], jnp.concatenate(fields, axis=0))
            wave_ref[layer + 1, pair] = ahead.astype(jnp.bfloat16)
        code_out(layer).start()
        return carry

    lax.fori_loop(0, slices, descend, 0)
    for layer in range(slices):
        code_out(layer).wait()


def ascend_kernel(
    offset_ref,
    table_hbm,
    amp_ref,
    codes_hbm,
    wave_ref,
    own_ref,
    other_ref,
    table_ref,
    code_ref,
    grad_ref,
    sum_ref,
    table_sem,
    code_sem,
):
    slices, count, extent, _ = code_ref.shape
    side = own_ref.shape[-1]
    pairs = count // 2
    pieces = amp_ref.shape[0]
    tall = extent + 8
    core = lax.axis_index("cuts") % 2

    def table_in(which):
        return pltpu.make_async_copy(
            table_hbm.at[pl.ds(2 * which, 2)], table_ref.at[pl.ds(2 * which, 2)], table_sem.at[which]
        )

    def code_in(layer):
        return pltpu.make_async_copy(codes_hbm.at[layer], code_ref.at[layer], code_sem.at[layer])

    table_in(1).start()
    table_in(0).start()
    for layer in reversed(range(slices)):
        code_in(layer).start()

    table_in(1).wait()
    for pair in range(pairs):
        far = both_sides(table_ref[2], table_ref[3], wave_ref[slices, pair])
        residue = []
        for item in range(2):
            position, rows = part(extent, pair, item)
            f_real, f_imag = far[rows, :extent], far[rows, extent:]
            amplitude = jnp.concatenate(
                [amp_ref[piece, position] for piece in range(pieces)], axis=0
            ).astype(jnp.float32)
            amp = jnp.sqrt(f_real * f_real + f_imag * f_imag + softening)
            ratio = (amp - amplitude) / amp
            residue.append(
                jnp.concatenate([ratio * f_real, ratio * f_imag], axis=1).astype(jnp.bfloat16)
            )
        back = both_sides(table_ref[3], table_ref[2], jnp.concatenate(residue, axis=0))
        grad_ref[pair] = back.astype(jnp.bfloat16)
    table_in(0).wait()

    def ascend(step, carry):
        layer = slices - 1 - step
        code_in(layer).wait()
        sum_ref[...] = jnp.zeros_like(sum_ref)
        for pair in range(pairs):
            back = both_sides(table_ref[1], table_ref[0], grad_ref[pair])
            for item in range(2):
                position, rows = part(extent, pair, item)
                u_real, u_imag = back[rows, :extent], back[rows, extent:]
                t_real, t_imag = decode(code_ref[layer, position])
                grad_ref[pair, rows, :extent] = (u_real * t_real + u_imag * t_imag).astype(jnp.bfloat16)
                grad_ref[pair, rows, extent:] = (u_imag * t_real - u_real * t_imag).astype(jnp.bfloat16)
                wave = wave_ref[layer, pair, rows, :].astype(jnp.float32)
                w_real, w_imag = wave[:, :extent], wave[:, extent:]
                col_at, row_at, down = placed(offset_ref, position, side, tall)
                for plane, contrib in enumerate(
                    (u_real * w_real + u_imag * w_imag, u_imag * w_real - u_real * w_imag)
                ):
                    high = jnp.concatenate(
                        [contrib, jnp.zeros((tall - extent, extent), jnp.float32)], axis=0
                    )
                    wide = jnp.concatenate(
                        [pltpu.roll(high, down, 0), jnp.zeros((tall, side - extent), jnp.float32)],
                        axis=1,
                    )
                    sum_ref[plane, pl.ds(row_at, tall), :] += pltpu.roll(wide, col_at, 1)
        mine = layer % 2 == core

        @pl.when(mine)
        def _():
            own_ref[layer // 2, :side] = sum_ref[0].astype(jnp.bfloat16)
            own_ref[layer // 2, side:] = sum_ref[1].astype(jnp.bfloat16)

        @pl.when(jnp.logical_not(mine))
        def _():
            other_ref[layer // 2, :side] = sum_ref[0].astype(jnp.bfloat16)
            other_ref[layer // 2, side:] = sum_ref[1].astype(jnp.bfloat16)

        return carry

    lax.fori_loop(0, slices, ascend, 0)


def in_hbm(array):
    return pltpu.with_memory_space_constraint(array, pltpu.HBM)


SMEM = pl.BlockSpec(memory_space=pltpu.SMEM)
VMEM = pl.BlockSpec(memory_space=pltpu.VMEM)
HBM = pl.BlockSpec(memory_space=pltpu.HBM)
FULL = 67_043_328


def leaving(room):
    return pltpu.CompilerParams(vmem_limit_bytes=FULL - room)


def small_call(kernel, shape, dtype, specs):
    return pl.pallas_call(
        kernel,
        out_shape=jax.ShapeDtypeStruct(shape, dtype),
        in_specs=specs,
        out_specs=VMEM,
        compiler_params=leaving(40 << 20),
    )


def forward(offsets, mine, theirs, probe_real, probe_imag, table, steps):
    chips, side, _ = mine.shape
    slices = 2 * chips
    extent = probe_real.shape[-1]
    count = offsets.shape[1] // lax.axis_size("cuts")
    square = (count // 2, 2 * extent, 2 * extent)
    return pl.pallas_call(
        functools.partial(descend_kernel, steps=steps),
        out_shape=(
            pltpu.HBM((slices, count, extent, extent), jnp.int32),
            jax.ShapeDtypeStruct((slices + 1,) + square, jnp.bfloat16),
        ),
        in_specs=[SMEM, HBM, HBM, HBM, VMEM, VMEM],
        out_specs=(HBM, VMEM),
        scratch_shapes=[
            pltpu.VMEM((2,) + table.shape[1:], table.dtype),
            pltpu.VMEM((slices, side, side), jnp.int32),
            pltpu.VMEM((slices, count, extent, extent), jnp.int32),
            pltpu.SemaphoreType.DMA,
            pltpu.SemaphoreType.DMA((slices,)),
            pltpu.SemaphoreType.DMA((slices,)),
        ],
        name="descend",
        compiler_params=leaving(40 << 20),
        cost_estimate=pl.CostEstimate(
            flops=2 * (slices + 1) * count * 8 * extent**3, bytes_accessed=6 << 20, transcendentals=0
        ),
    )(offsets, in_hbm(mine), in_hbm(theirs), in_hbm(table), probe_real, probe_imag)


def backward(offsets, table, amp_pieces, codes, waves, side):
    slices, count, extent, _ = codes.shape
    half = jax.ShapeDtypeStruct((slices // 2, 2 * side, side), jnp.bfloat16)
    square = (count // 2, 2 * extent, 2 * extent)
    return pl.pallas_call(
        ascend_kernel,
        out_shape=(half, half),
        in_specs=[SMEM, HBM, VMEM, HBM, VMEM],
        out_specs=(VMEM, VMEM),
        scratch_shapes=[
            pltpu.VMEM(table.shape, table.dtype),
            pltpu.VMEM((slices, count, extent, extent), jnp.int32),
            pltpu.VMEM(square, jnp.bfloat16),
            pltpu.VMEM((2, side, side), jnp.float32),
            pltpu.SemaphoreType.DMA((2,)),
            pltpu.SemaphoreType.DMA((slices,)),
        ],
        name="ascend",
        compiler_params=leaving(40 << 20),
        cost_estimate=pl.CostEstimate(
            flops=2 * (slices + 1) * count * 8 * extent**3, bytes_accessed=6 << 20, transcendentals=0
        ),
    )(offsets, in_hbm(table), amp_pieces, in_hbm(codes), waves)


def fetch_patterns(pattern_index, measured, sections):
    positions, extent, _ = measured.shape
    tile_count = lax.axis_size("tile")
    share = extent // sections
    ask = functools.partial(ask_kernel, stored=positions)
    request = small_call(ask, (tile_count, 1, 128), jnp.int32, [SMEM])(pattern_index)
    requested = lax.all_to_all(request, "tile", split_axis=0, concat_axis=0, tiled=True)
    first = lax.axis_index("cuts") * share
    shares = lax.dynamic_slice_in_dim(measured, first, share, 1)
    block = (share, extent)
    rows = small_call(pick_kernel, (tile_count,) + block, measured.dtype, [SMEM, VMEM])(
        requested, shares
    )
    answered = lax.all_to_all(rows, "tile", split_axis=0, concat_axis=0, tiled=True)
    sort = functools.partial(sort_kernel, stored=positions)
    pieces = small_call(sort, (positions,) + block, measured.dtype, [SMEM, VMEM])(
        pattern_index, answered
    )
    pieces = pieces.reshape(sections, positions // sections, share, extent)
    return lax.all_to_all(pieces, "cuts", split_axis=0, concat_axis=0, tiled=True)


def across(chips, step):
    return [(2 * at + core, 2 * ((at + step) % chips) + core) for at in range(chips) for core in range(2)]


def local(trans_real, trans_imag, probe_real, probe_imag, offsets, pattern_index, measured):
    extent = probe_real.shape[-1]
    side = trans_real.shape[-1]
    sections = lax.axis_size("cuts")
    chips = sections // 2
    sibling = [(at, at ^ 1) for at in range(sections)]
    steps = [0] + sorted(range(1, chips), key=lambda step: min(step, chips - step))

    table = jnp.asarray(tables(extent))
    amp_pieces = fetch_patterns(pattern_index, measured, sections)
    code = encode(trans_real, trans_imag)
    mine = [code]
    for step in steps[1:]:
        mine.append(lax.ppermute(code, "cuts", across(chips, step)))
    mine = jnp.concatenate(mine, axis=0)
    theirs = lax.ppermute(mine, "cuts", sibling)
    codes, waves = forward(offsets, mine, theirs, probe_real, probe_imag, table, steps)
    own, other = backward(offsets, table, amp_pieces, codes, waves, side)
    met = lax.ppermute(other, "cuts", sibling)
    paired = (own.astype(jnp.float32) + met.astype(jnp.float32)).astype(jnp.bfloat16)
    groups = [[2 * at + parity for at in range(chips)] for parity in range(2)]
    parts = lax.all_to_all(
        paired, "cuts", split_axis=0, concat_axis=0, tiled=True, axis_index_groups=groups
    )
    total = jnp.sum(parts.astype(jnp.float32), axis=0)
    return total.reshape(2, 1, side, side)


def solution(mesh):
    return jax.shard_map(
        local,
        mesh=mesh,
        in_specs=(
            P("cuts", "tile", None),
            P("cuts", "tile", None),
            P(),
            P(),
            P(None, "tile"),
            P("tile"),
            P("tile", None, None),
        ),
        out_specs=P(None, "cuts", "tile", None),
        check_vma=False,
    )
```
